256 devices in a mesh: region: 4 (over x_hi, core), shard: 64 (over y, x_lo, z).
Axes of the slice: x: 4 (x_hi: 2, x_lo: 2; x = x_hi * 2 + x_lo), y: 4, z: 8, core: 2. Of those that a mesh axis runs over, the one named last changes fastest.
Arguments:
- region_role: int32 [4], replicated, may hold values from 0 to 3, each once
- tokens: bfloat16 [8192, 5120], P(('region', 'shard')), may hold values from -6 to 6
- cotangent: bfloat16 [8192, 16384], P('region', 'shard'), may hold values from -0.125 to 0.125
- master: float32 [5120, 16384], P('region', 'shard'), may hold values from -3 to 3
- momentum: float32 [5120, 16384], P('region', 'shard'), may hold values from -6 to 6
Outputs:
- new_master: float32 [5120, 16384], P('region', 'shard')
- new_momentum: float32 [5120, 16384], P('region', 'shard')
- learner_weight: bfloat16 [5120, 16384], P(None, 'shard')
- rollout_weight: bfloat16 [4, 1280, 16384], P(None, 'shard')
The draws below stay inside these ranges and needn't reach their ends.
Inputs may be any that keep to these rules, and one draw needn't show every extreme that they name: `region_role`: the two regions holding 0 and 1 form the larger learner group, the region holding 2 is the smaller learner group, the region holding 3 serves rollout; each value appears once.
All inputs are finite; a program needn't handle non-finite values.
Results may differ from the reference program's by a relative error of at most 0.001.
Values may be sent and summed in bfloat16 or wider, within the bound.
No kernel may reach another device: no remote copies, remote signals or barrier semaphores. Data moves between devices by JAX's collectives and lax.ppermute only.
A program may use at most 128 MiB of HBM per device.

```python
import jax
import jax.numpy as jnp
from jax import lax

D = 5120
FF = 16384
TOK_REGION = 2048
TOKENS = 8192
N_REGION = 4


def level_of(rng, dims, pieces, least, top_value):
    level = 1.0
    for axis_at, parts in pieces:
        steps = jax.random.uniform(jax.random.fold_in(jax.random.fold_in(rng, 6), axis_at), (parts,), jnp.float32, least / len(pieces), top_value / len(pieces))
        level = level * jnp.repeat(jnp.exp(steps), dims[axis_at] // parts).reshape((-1,) + (1,) * (len(dims) - 1 - axis_at))
    return level


def noise(key, extent, deviation, most, cuts=(), kind=jnp.bfloat16):
    drawn = jax.random.normal(key, extent, jnp.float32) * deviation
    if len(cuts) > 0:
        drawn = level_of(key, extent, cuts, -0.22, 0.18) * drawn
    return jnp.clip(drawn, min=-most, max=most).astype(kind)


def setup_inputs(seed: int = 0) -> dict:
    key_of = jax.random.split(jax.random.key(seed), 6)
    region_role = jax.random.permutation(key_of[0], N_REGION).astype(jnp.int32)
    tokens = noise(key_of[1], (TOKENS, D), 1.0, 6.0, ((0, 256),))
    cotangent = noise(key_of[2], (TOKENS, FF), TOK_REGION ** -0.5, 0.125, ((0, 4), (1, 64)))
    master = noise(key_of[3], (D, FF), 0.5, 3.0, ((0, 4), (1, 64)), jnp.float32)
    momentum = noise(key_of[4], (D, FF), 1.0, 6.0, ((0, 4), (1, 64)), jnp.float32)
    return dict(region_role=region_role, tokens=tokens, cotangent=cotangent, master=master, momentum=momentum)


def reference(region_role, tokens, cotangent, master, momentum):
    share = jnp.where(region_role < 2, 0.25, jnp.where(region_role == 2, 0.5, 0.0)).astype(jnp.float32)
    delta = jnp.zeros((D, FF), jnp.float32)
    for region in range(N_REGION):
        inputs = tokens[region * TOK_REGION:(region + 1) * TOK_REGION]
        cotan = cotangent[region * TOK_REGION:(region + 1) * TOK_REGION]
        grad = lax.dot_general(inputs, cotan, (((0,), (0,)), ((), ())), preferred_element_type=jnp.float32)
        delta = delta + share[region] * grad
    new_momentum = 0.9 * momentum + delta
    new_master = master - 0.7 * (delta + 0.9 * new_momentum)
    learner_weight = new_master.astype(jnp.bfloat16)
    rollout_weight = learner_weight.reshape(N_REGION, D // N_REGION, FF)
    return new_master, new_momentum, learner_weight, rollout_weight
```

```python
import functools

import jax
import jax.numpy as jnp
from jax import lax
from jax.experimental import pallas as pl
from jax.experimental.pallas import tpu as pltpu
from jax.sharding import Mesh, PartitionSpec as P

REGION = ("xh", "core")
SHARD = ("y", "xl", "z")
WIDE = 384


def shift(x, axis, n, by):
    return lax.ppermute(x, axis, [(i, (i + by) % n) for i in range(n)])


def ring(x, axis, n, half_axis):
    out = [None] * n
    out[0] = up = down = x
    for k in range(1, n // 2):
        up, down = shift(up, axis, n, 1), shift(down, axis, n, -1)
        out[n - k], out[k] = up, down
    half = x.shape[half_axis] // 2
    far = (
        shift(lax.slice_in_dim(up, 0, half, axis=half_axis), axis, n, 1),
        shift(lax.slice_in_dim(down, half, 2 * half, axis=half_axis), axis, n, -1),
    )
    out[n // 2] = jnp.concatenate(far, half_axis)
    return out


def gradient_kernel(ny, nz, *refs):
    wide, narrow, cot = refs[:ny], refs[ny : ny + nz], refs[ny + nz]
    own, other = refs[ny + nz + 1 :]
    mine = lax.axis_index("xl")
    for out, column in ((own, mine), (other, 1 - mine)):
        first = True
        for j in range(ny):
            for r in range(4):
                part = lax.dot_general(
                    wide[j][r], cot[2 * r + column, j].reshape(512, 256), (((0,), (0,)), ((), ())),
                    preferred_element_type=jnp.float32)
                if first:
                    out[:WIDE, :] = part
                    first = False
                else:
                    out[:WIDE, :] += part
        first = True
        for m in range(nz):
            for r in range(4):
                rows = jnp.concatenate(
                    [cot[2 * r + column, j, l, m] for j in range(ny) for l in range(2)], 0)
                part = lax.dot_general(
                    narrow[m][r], rows, (((0,), (0,)), ((), ())), preferred_element_type=jnp.float32)
                if first:
                    out[WIDE:, :] = part
                    first = False
                else:
                    out[WIDE:, :] += part


def gradient(wide, narrow, cot):
    ny, nz = len(wide), len(narrow)
    tile = jax.ShapeDtypeStruct((640, 256), jnp.float32)
    return pl.pallas_call(
        functools.partial(gradient_kernel, ny, nz),
        out_shape=(tile, tile),
        in_specs=[pl.BlockSpec(memory_space=pltpu.VMEM)] * (ny + nz + 1),
        out_specs=[pl.BlockSpec(memory_space=pltpu.VMEM)] * 2,
        compiler_params=pltpu.CompilerParams(vmem_limit_bytes=40 << 20),
        cost_estimate=pl.CostEstimate(flops=2 * 8192 * 640 * 512, bytes_accessed=20 << 20, transcendentals=0),
        name="gradient",
    )(*wide, *narrow, cot)


def roll_to(x, axis, start):
    return lax.dynamic_slice_in_dim(jnp.concatenate([x, x], axis), start, x.shape[axis], axis)


def per_device(region_role, tokens, cotangent, master, momentum):
    role = region_role[lax.axis_index(REGION)]
    share = jnp.where(role < 2, 0.25, jnp.where(role == 2, 0.5, 0.0)).astype(tokens.dtype)
    y, z, low = lax.axis_index("y"), lax.axis_index("z"), lax.axis_index("xl")

    cot = cotangent.reshape(4, 2, 8, 32, 256)
    cot = roll_to(roll_to(cot, 0, y), 2, z)
    cots = lax.all_gather(cot.reshape(2048, 256), ("xh", "core", "xl"), axis=0, tiled=True)
    cots = cots.reshape(8, 4, 2, 8, 32, 256)

    blocks = (tokens * share).reshape(32, 8, 640).transpose(1, 0, 2)
    here = lax.all_to_all(blocks, ("xh", "core", "xl"), split_axis=0, concat_axis=0, tiled=True)
    wide = [t[:, None] for t in ring(here[:, :, :WIDE], "z", 8, 1)]
    wide = jnp.concatenate(wide, 1)
    narrow = [t.reshape(4, 1, 2, 32, 640 - WIDE) for t in ring(here[:, :, WIDE:], "y", 4, 1)]
    narrow = jnp.concatenate(narrow, 1)
    wide = [t.reshape(4, 512, WIDE) for t in ring(wide, "y", 4, 0)]
    narrow = [t.reshape(4, 256, 640 - WIDE) for t in ring(narrow, "z", 8, 0)]

    own, other = gradient(wide, narrow, cots)
    came = shift(other, "xl", 2, 1)
    delta = jnp.where(low == 0, jnp.concatenate([own, came], 0), jnp.concatenate([came, own], 0))

    new_momentum = 0.9 * momentum + delta
    new_master = master - 0.7 * (delta + 0.9 * new_momentum)
    fresh = new_master.astype(jnp.bfloat16)
    learner_weight = lax.all_gather(fresh, REGION, axis=0, tiled=True)
    rows = lax.all_to_all(fresh.reshape(64, 20, 256), SHARD, split_axis=0, concat_axis=0, tiled=True)
    rows = rows.transpose(1, 0, 2).reshape(20, 16384)
    rollout_weight = lax.all_gather(rows, REGION, axis=0, tiled=False)
    return new_master, new_momentum, learner_weight, rollout_weight


def solution(mesh):
    fine = Mesh(mesh.devices.reshape(2, 2, 4, 2, 8), REGION + SHARD)
    tile = P(REGION, SHARD)
    return jax.shard_map(
        per_device,
        mesh=fine,
        in_specs=(P(), P(REGION + SHARD, None), tile, tile, tile),
        out_specs=(tile, tile, P(None, SHARD), P(None, SHARD, None)),
        check_vma=False,
    )
```

```python
import functools

import jax
import jax.numpy as jnp
from jax import lax
from jax.experimental import pallas as pl
from jax.experimental.pallas import tpu as pltpu
from jax.sharding import Mesh, PartitionSpec as P

REGION = ("xh", "core")
SHARD = ("y", "xl", "z")
WIDE = 384
NARROW = 256


def shift(x, axis, n, by):
    return lax.ppermute(x, axis, [(i, (i + by) % n) for i in range(n)])


def both(pair, axis, n):
    return shift(pair[0], axis, n, 1), shift(pair[1], axis, n, -1)


def halves(pair, axis, n, dim):
    size = pair[0].shape[dim] // 2
    return both(
        (lax.slice_in_dim(pair[0], 0, size, axis=dim), lax.slice_in_dim(pair[1], size, 2 * size, axis=dim)),
        axis, n)


def after(values, others):
    return lax.optimization_barrier((values, others))[0]


def gradient_kernel(js, ms, first, last, *refs):
    role, refs = refs[0], refs[1:]
    wide, refs = refs[: len(js)], refs[len(js) :]
    narrow, refs = refs[: len(ms)], refs[len(ms) :]
    cots, refs = refs[0], refs[1:]
    before, refs = ((), refs) if first else (refs[:2], refs[2:])
    old, refs = (refs[:2], refs[2:]) if last else ((), refs)
    low = lax.axis_index("xl")
    ys = [lax.rem(lax.axis_index("y") + j, 4) for j in range(4)]
    zs = [lax.rem(lax.axis_index("z") + m, 8) for m in range(8)]
    shares = [jnp.where(role[r] < 2, 0.25, jnp.where(role[r] == 2, 0.5, 0.0)) for r in range(4)]
    for side in range(2):
        column = low if side == 0 else 1 - low
        sources = [(cots.at[region // 2, column, region % 2], region) for region in range(4)]
        total = None if first else before[side][:WIDE, :]
        for cot, region in sources:
            for ref, j in zip(wide, js):
                rows = jnp.concatenate([cot[ys[j], l, zs[m]] for l in range(2) for m in range(8)], 0)
                part = shares[region] * lax.dot_general(
                    ref[region], rows, (((0,), (0,)), ((), ())), preferred_element_type=jnp.float32)
                total = part if total is None else total + part
        refs[side][:WIDE, :] = total
        total = None if first else before[side][WIDE:, :]
        for cot, region in sources:
            for ref, m in zip(narrow, ms):
                rows = jnp.concatenate([cot[ys[j], l, zs[m]] for j in range(4) for l in range(2)], 0)
                part = shares[region] * lax.dot_general(
                    ref[region], rows, (((0,), (0,)), ((), ())), preferred_element_type=jnp.float32)
                total = part if total is None else total + part
        refs[side][WIDE:, :] = total
        if last:
            for target in range(32):
                at = slice(20 * target, 20 * target + 20)
                new = step(refs[side][at, :], old[side][0, at, :], old[side][1, at, :])[0]
                refs[2][target, column] = new.astype(jnp.bfloat16)


def gradient(role, wide, narrow, cots, before=(), old=()):
    js, ms = tuple(wide), tuple(narrow)
    tile = jax.ShapeDtypeStruct((640, 256), jnp.float32)
    rows = jax.ShapeDtypeStruct((32, 2, 20, 256), jnp.bfloat16)
    operands = (role, *wide.values(), *narrow.values(), cots, *before, *old)
    at = len(operands) - len(before) - len(old)
    share = (len(js) / 4 * WIDE + len(ms) / 8 * NARROW) / 640
    return pl.pallas_call(
        functools.partial(gradient_kernel, js, ms, not before, bool(old)),
        out_shape=(tile, tile, rows) if old else (tile, tile),
        in_specs=[pl.BlockSpec(memory_space=pltpu.SMEM)]
        + [pl.BlockSpec(memory_space=pltpu.VMEM)] * (len(operands) - 1),
        out_specs=[pl.BlockSpec(memory_space=pltpu.VMEM)] * (3 if old else 2),
        input_output_aliases={at: 0, at + 1: 1} if before else {},
        compiler_params=pltpu.CompilerParams(vmem_limit_bytes=8 << 20),
        cost_estimate=pl.CostEstimate(
            flops=int(share * 2 * 8192 * 640 * 512), bytes_accessed=int(share * (18 << 20)), transcendentals=0),
        name="gradient",
    )(*operands)


def step(delta, master, momentum):
    new_momentum = 0.9 * momentum + delta
    return master - 0.7 * (delta + 0.9 * new_momentum), new_momentum


def in_order(low, own, other, axis):
    return jnp.where(low == 0, jnp.stack([own, other], axis), jnp.stack([other, own], axis))


def per_device(region_role, tokens, cotangent, master, momentum):
    low, core = lax.axis_index("xl"), lax.axis_index("core")

    blocks = tokens.reshape(32, 4, 4, 2, 160).transpose(1, 3, 0, 2, 4).reshape(8, 32, 640)
    here = lax.all_to_all(blocks, ("xh", "core", "xl"), split_axis=0, concat_axis=0, tiled=True)
    a0, b0 = here[:, :, :WIDE], here[:, :, WIDE:]

    cots = lax.all_gather(cotangent, ("xh", "xl", "core"), axis=0, tiled=True).reshape(2, 2, 2, 4, 2, 8, 32, 256)

    a1, b1 = both((a0, a0), "z", 8), both((b0, b0), "y", 4)
    a1, b1 = lax.optimization_barrier((a1, b1))
    a2, b2 = both(a1, "z", 8), halves(b1, "y", 4, 1)
    a2, b2 = lax.optimization_barrier((a2, b2))
    a3 = both(a2, "z", 8)
    narrow = [b0, b1[1], jnp.concatenate(b2, 1), b1[0]]
    narrow = jnp.concatenate([t.reshape(4, 1, 2, 32, NARROW) for t in narrow], 1)
    a3, narrow = lax.optimization_barrier((a3, narrow))
    a4 = halves(a3, "z", 8, 1)
    n1 = both((narrow, narrow), "z", 8)
    wide = [a0, a1[1], a2[1], a3[1], jnp.concatenate(a4, 1), a3[0], a2[0], a1[0]]
    wide = jnp.concatenate([t[:, None] for t in wide], 1)
    w1 = both((wide, wide), "y", 4)

    old = jnp.stack([master, momentum]).reshape(2, 4, 2, 160, 256)
    mine = lax.dynamic_index_in_dim(old, low, 2, keepdims=False)
    theirs = shift(after(lax.dynamic_index_in_dim(old, 1 - low, 2, keepdims=False), narrow), "xl", 2, 1)
    mine, theirs = mine.reshape(2, 640, 256), theirs.reshape(2, 640, 256)

    n2 = both(n1, "z", 8)
    w1, theirs = lax.optimization_barrier((w1, theirs))
    w2 = halves(w1, "y", 4, 0)
    n3 = both(n2, "z", 8)
    shaped = lambda t: t.reshape(4, -1, t.shape[-1])
    tile = gradient(
        region_role,
        {0: shaped(wide), 1: shaped(w1[1]), 3: shaped(w1[0])},
        {0: shaped(narrow), 1: shaped(n1[1]), 7: shaped(n1[0]), 2: shaped(n2[1]), 6: shaped(n2[0])}, cots)
    n3, tile = lax.optimization_barrier((n3, tile))
    n4 = halves(n3, "z", 8, 0)
    own, other, rows = gradient(
        region_role,
        {2: shaped(jnp.concatenate(w2, 0))},
        {3: shaped(n3[1]), 5: shaped(n3[0]), 4: shaped(jnp.concatenate(n4, 0))}, cots, tile, (mine, theirs))

    came = shift(other, "xl", 2, 1)
    rows = lax.all_to_all(rows, ("y", "z"), split_axis=0, concat_axis=0, tiled=True)
    rows = rows.reshape(4, 8, 2, 20, 256).transpose(3, 0, 2, 1, 4).reshape(20, 16384)
    far = shift(rows, "xh", 2, 1)
    near = shift(rows, "core", 2, 1)
    far_near = shift(far, "core", 2, 1)
    rollout_weight = in_order(
        lax.axis_index("xh"), in_order(core, rows, near, 0), in_order(core, far, far_near, 0), 0)
    rollout_weight = rollout_weight.reshape(4, 20, 16384)

    delta = in_order(low, own.reshape(4, 160, 256), came.reshape(4, 160, 256), 1).reshape(1280, 256)
    new_master, new_momentum = step(delta, master, momentum)
    fresh = new_master.astype(jnp.bfloat16)
    learner_weight = lax.all_gather(fresh, REGION, axis=0, tiled=True)
    return new_master, new_momentum, learner_weight, rollout_weight


def solution(mesh):
    fine = Mesh(mesh.devices.reshape(2, 2, 4, 2, 8), REGION + SHARD)
    tile = P(REGION, SHARD)
    return jax.shard_map(
        per_device,
        mesh=fine,
        in_specs=(P(), P(REGION + SHARD, None), tile, tile, tile),
        out_specs=(tile, tile, P(None, SHARD), P(None, SHARD, None)),
        check_vma=False,
    )
```

```python
import functools

import jax
import jax.numpy as jnp
from jax import lax
from jax.experimental import pallas as pl
from jax.experimental.pallas import tpu as pltpu
from jax.sharding import Mesh, PartitionSpec as P

REGION = ("xh", "core")
SHARD = ("y", "xl", "z")
WIDE = 384
NARROW = 256


def shift(x, axis, n, by):
    return lax.ppermute(x, axis, [(i, (i + by) % n) for i in range(n)])


def both(pair, axis, n):
    return shift(pair[0], axis, n, 1), shift(pair[1], axis, n, -1)


def halves(pair, axis, n, dim):
    size = pair[0].shape[dim] // 2
    return both(
        (lax.slice_in_dim(pair[0], 0, size, axis=dim), lax.slice_in_dim(pair[1], size, 2 * size, axis=dim)),
        axis, n)


def after(values, others):
    return lax.optimization_barrier((values, others))[0]


def gradient_kernel(js, ms, first, last, *refs):
    role, refs = refs[0], refs[1:]
    wide, refs = refs[: len(js)], refs[len(js) :]
    narrow, refs = refs[: len(ms)], refs[len(ms) :]
    cots, refs = refs[0], refs[1:]
    before, refs = ((), refs) if first else (refs[:2], refs[2:])
    old, refs = (refs[:2], refs[2:]) if last else ((), refs)
    low = lax.axis_index("xl")
    ys = [lax.rem(lax.axis_index("y") + j, 4) for j in range(4)]
    zs = [lax.rem(lax.axis_index("z") + m, 8) for m in range(8)]
    shares = [jnp.where(role[r] < 2, 0.25, jnp.where(role[r] == 2, 0.5, 0.0)) for r in range(4)]
    for side in range(2):
        column = low if side == 0 else 1 - low
        sources = [(cots.at[region // 2, column, region % 2], region) for region in range(4)]
        total = None if first else before[side][:WIDE, :]
        for cot, region in sources:
            for ref, j in zip(wide, js):
                rows = jnp.concatenate([cot[ys[j], l, zs[m]] for l in range(2) for m in range(8)], 0)
                part = shares[region] * lax.dot_general(
                    ref[region], rows, (((0,), (0,)), ((), ())), preferred_element_type=jnp.float32)
                total = part if total is None else total + part
        refs[side][:WIDE, :] = total
        total = None if first else before[side][WIDE:, :]
        for cot, region in sources:
            for ref, m in zip(narrow, ms):
                rows = jnp.concatenate([cot[ys[j], l, zs[m]] for j in range(4) for l in range(2)], 0)
                part = shares[region] * lax.dot_general(
                    ref[region], rows, (((0,), (0,)), ((), ())), preferred_element_type=jnp.float32)
                total = part if total is None else total + part
        refs[side][WIDE:, :] = total
        if last:
            for target in range(32):
                at = slice(20 * target, 20 * target + 20)
                new = step(refs[side][at, :], old[side][0, at, :], old[side][1, at, :])[0]
                refs[2][target, column] = new.astype(jnp.bfloat16)


def gradient(role, wide, narrow, cots, before=(), old=()):
    js, ms = tuple(wide), tuple(narrow)
    tile = jax.ShapeDtypeStruct((640, 256), jnp.float32)
    rows = jax.ShapeDtypeStruct((32, 2, 20, 256), jnp.bfloat16)
    operands = (role, *wide.values(), *narrow.values(), cots, *before, *old)
    at = len(operands) - len(before) - len(old)
    share = (len(js) / 4 * WIDE + len(ms) / 8 * NARROW) / 640
    return pl.pallas_call(
        functools.partial(gradient_kernel, js, ms, not before, bool(old)),
        out_shape=(tile, tile, rows) if old else (tile, tile),
        in_specs=[pl.BlockSpec(memory_space=pltpu.SMEM)]
        + [pl.BlockSpec(memory_space=pltpu.VMEM)] * (len(operands) - 1),
        out_specs=[pl.BlockSpec(memory_space=pltpu.VMEM)] * (3 if old else 2),
        input_output_aliases={at: 0, at + 1: 1} if before else {},
        compiler_params=pltpu.CompilerParams(vmem_limit_bytes=8 << 20),
        cost_estimate=pl.CostEstimate(
            flops=int(share * 2 * 8192 * 640 * 512), bytes_accessed=int(share * (18 << 20)), transcendentals=0),
        name="gradient",
    )(*operands)


def step(delta, master, momentum):
    new_momentum = 0.9 * momentum + delta
    return master - 0.7 * (delta + 0.9 * new_momentum), new_momentum


def in_order(low, own, other, axis):
    return jnp.where(low == 0, jnp.stack([own, other], axis), jnp.stack([other, own], axis))


def every_region(block, axis):
    far, near = shift(block, "xh", 2, 1), shift(block, "core", 2, 1)
    far_near = shift(far, "core", 2, 1)
    core = lax.axis_index("core")
    return in_order(lax.axis_index("xh"), in_order(core, block, near, axis), in_order(core, far, far_near, axis), axis)


def per_device(region_role, tokens, cotangent, master, momentum):
    low, core = lax.axis_index("xl"), lax.axis_index("core")

    blocks = tokens.reshape(32, 4, 4, 2, 160).transpose(1, 3, 0, 2, 4).reshape(8, 32, 640)
    here = lax.all_to_all(blocks, ("xh", "core", "xl"), split_axis=0, concat_axis=0, tiled=True)
    a0, b0 = here[:, :, :WIDE], here[:, :, WIDE:]

    cots = lax.all_gather(cotangent, ("xh", "xl", "core"), axis=0, tiled=True).reshape(2, 2, 2, 4, 2, 8, 32, 256)

    a1, b1 = both((a0, a0), "z", 8), both((b0, b0), "y", 4)
    a1, b1 = lax.optimization_barrier((a1, b1))
    a2, b2 = both(a1, "z", 8), halves(b1, "y", 4, 1)
    a2, b2 = lax.optimization_barrier((a2, b2))
    a3 = both(a2, "z", 8)
    narrow = [b0, b1[1], jnp.concatenate(b2, 1), b1[0]]
    narrow = jnp.concatenate([t.reshape(4, 1, 2, 32, NARROW) for t in narrow], 1)
    a3, narrow = lax.optimization_barrier((a3, narrow))
    a4 = halves(a3, "z", 8, 1)
    n1 = both((narrow, narrow), "z", 8)
    wide = [a0, a1[1], a2[1], a3[1], jnp.concatenate(a4, 1), a3[0], a2[0], a1[0]]
    wide = jnp.concatenate([t[:, None] for t in wide], 1)
    w1 = both((wide, wide), "y", 4)

    old = jnp.stack([master, momentum]).reshape(2, 4, 2, 160, 256)
    mine = lax.dynamic_index_in_dim(old, low, 2, keepdims=False)
    theirs = shift(after(lax.dynamic_index_in_dim(old, 1 - low, 2, keepdims=False), narrow), "xl", 2, 1)
    mine, theirs = mine.reshape(2, 640, 256), theirs.reshape(2, 640, 256)

    n2 = both(n1, "z", 8)
    w2 = halves(w1, "y", 4, 0)
    n3 = both(n2, "z", 8)
    shaped = lambda t: t.reshape(4, -1, t.shape[-1])
    tile = gradient(
        region_role,
        {0: shaped(wide), 1: shaped(w1[1]), 3: shaped(w1[0])},
        {0: shaped(narrow), 1: shaped(n1[1]), 7: shaped(n1[0]), 2: shaped(n2[1]), 6: shaped(n2[0])}, cots)
    n3, tile, theirs = lax.optimization_barrier((n3, tile, theirs))
    n4 = halves(n3, "z", 8, 0)
    own, other, rows = gradient(
        region_role,
        {2: shaped(jnp.concatenate(w2, 0))},
        {3: shaped(n3[1]), 5: shaped(n3[0]), 4: shaped(jnp.concatenate(n4, 0))}, cots, tile, (mine, theirs))

    came = shift(other, "xl", 2, 1)
    rows = lax.all_to_all(rows, ("y", "z"), split_axis=0, concat_axis=0, tiled=True)
    rows = rows.reshape(4, 8, 2, 20, 256).transpose(3, 0, 2, 1, 4).reshape(20, 16384)
    rollout_weight = every_region(rows, 0).reshape(4, 20, 16384)

    delta = in_order(low, own.reshape(4, 160, 256), came.reshape(4, 160, 256), 1).reshape(1280, 256)
    new_master, new_momentum = step(delta, master, momentum)
    learner_weight = every_region(new_master.astype(jnp.bfloat16), 0).reshape(5120, 256)
    return new_master, new_momentum, learner_weight, rollout_weight


def solution(mesh):
    fine = Mesh(mesh.devices.reshape(2, 2, 4, 2, 8), REGION + SHARD)
    tile = P(REGION, SHARD)
    return jax.shard_map(
        per_device,
        mesh=fine,
        in_specs=(P(), P(REGION + SHARD, None), tile, tile, tile),
        out_specs=(tile, tile, P(None, SHARD), P(None, SHARD, None)),
        check_vma=False,
    )
```

```python
import functools

import jax
import jax.numpy as jnp
from jax import lax
from jax.experimental import pallas as pl
from jax.experimental.pallas import tpu as pltpu
from jax.sharding import Mesh, PartitionSpec as P

REGION = ("xh", "core")
SHARD = ("y", "xl", "z")
WIDE = 384
NARROW = 256


def shift(x, axis, n, by):
    return lax.ppermute(x, axis, [(i, (i + by) % n) for i in range(n)])


def both(pair, axis, n):
    return shift(pair[0], axis, n, 1), shift(pair[1], axis, n, -1)


def halves(pair, axis, n, dim):
    size = pair[0].shape[dim] // 2
    return both(
        (lax.slice_in_dim(pair[0], 0, size, axis=dim), lax.slice_in_dim(pair[1], size, 2 * size, axis=dim)),
        axis, n)


def after(values, others):
    return lax.optimization_barrier((values, others))[0]


def gradient_kernel(js, ms, first, last, *refs):
    role, refs = refs[0], refs[1:]
    wide, refs = refs[: len(js)], refs[len(js) :]
    narrow, refs = refs[: len(ms)], refs[len(ms) :]
    cots, refs = refs[0], refs[1:]
    before, refs = ((), refs) if first else (refs[:2], refs[2:])
    old, refs = (refs[:2], refs[2:]) if last else ((), refs)
    low = lax.axis_index("xl")
    ys = [lax.rem(lax.axis_index("y") + j, 4) for j in range(4)]
    zs = [lax.rem(lax.axis_index("z") + m, 8) for m in range(8)]
    shares = [jnp.where(role[r] < 2, 0.25, jnp.where(role[r] == 2, 0.5, 0.0)) for r in range(4)]
    for side in range(2):
        column = low if side == 0 else 1 - low
        sources = [(cots.at[region // 2, column, region % 2], region) for region in range(4)]
        total = None if first else before[side][:WIDE, :]
        for cot, region in sources:
            for ref, j in zip(wide, js):
                rows = jnp.concatenate([cot[ys[j], l, zs[m]] for l in range(2) for m in range(8)], 0)
                part = shares[region] * lax.dot_general(
                    ref[region], rows, (((0,), (0,)), ((), ())), preferred_element_type=jnp.float32)
                total = part if total is None else total + part
        refs[side][:WIDE, :] = total
        total = None if first else before[side][WIDE:, :]
        for cot, region in sources:
            for ref, m in zip(narrow, ms):
                rows = jnp.concatenate([cot[ys[j], l, zs[m]] for j in range(4) for l in range(2)], 0)
                part = shares[region] * lax.dot_general(
                    ref[region], rows, (((0,), (0,)), ((), ())), preferred_element_type=jnp.float32)
                total = part if total is None else total + part
        refs[side][WIDE:, :] = total
        if last:
            for target in range(32):
                at = slice(20 * target, 20 * target + 20)
                new = step(refs[side][at, :], old[side][0, at, :], old[side][1, at, :])[0]
                refs[2][target, column] = new.astype(jnp.bfloat16)


def gradient(role, wide, narrow, cots, before=(), old=()):
    js, ms = tuple(wide), tuple(narrow)
    tile = jax.ShapeDtypeStruct((640, 256), jnp.float32)
    rows = jax.ShapeDtypeStruct((32, 2, 20, 256), jnp.bfloat16)
    operands = (role, *wide.values(), *narrow.values(), cots, *before, *old)
    at = len(operands) - len(before) - len(old)
    share = (len(js) / 4 * WIDE + len(ms) / 8 * NARROW) / 640
    return pl.pallas_call(
        functools.partial(gradient_kernel, js, ms, not before, bool(old)),
        out_shape=(tile, tile, rows) if old else (tile, tile),
        in_specs=[pl.BlockSpec(memory_space=pltpu.SMEM)]
        + [pl.BlockSpec(memory_space=pltpu.VMEM)] * (len(operands) - 1),
        out_specs=[pl.BlockSpec(memory_space=pltpu.VMEM)] * (3 if old else 2),
        input_output_aliases={at: 0, at + 1: 1} if before else {},
        compiler_params=pltpu.CompilerParams(vmem_limit_bytes=8 << 20),
        cost_estimate=pl.CostEstimate(
            flops=int(share * 2 * 8192 * 640 * 512), bytes_accessed=int(share * (18 << 20)), transcendentals=0),
        name="gradient",
    )(*operands)


def step(delta, master, momentum):
    new_momentum = 0.9 * momentum + delta
    return master - 0.7 * (delta + 0.9 * new_momentum), new_momentum


def in_order(low, own, other, axis):
    return jnp.where(low == 0, jnp.stack([own, other], axis), jnp.stack([other, own], axis))


def every_region(block, axis):
    far, near = shift(block, "xh", 2, 1), shift(block, "core", 2, 1)
    far_near = shift(far, "core", 2, 1)
    core = lax.axis_index("core")
    return in_order(lax.axis_index("xh"), in_order(core, block, near, axis), in_order(core, far, far_near, axis), axis)


def per_device(region_role, tokens, cotangent, master, momentum):
    low, core = lax.axis_index("xl"), lax.axis_index("core")

    blocks = tokens.reshape(32, 4, 4, 2, 160).transpose(1, 3, 0, 2, 4).reshape(8, 32, 640)
    here = lax.all_to_all(blocks, ("xh", "core", "xl"), split_axis=0, concat_axis=0, tiled=True)
    a0, b0 = here[:, :, :WIDE], here[:, :, WIDE:]

    cots = lax.all_gather(cotangent, ("xh", "xl", "core"), axis=0, tiled=True).reshape(2, 2, 2, 4, 2, 8, 32, 256)

    a1, b1 = both((a0, a0), "z", 8), both((b0, b0), "y", 4)
    a1, b1 = lax.optimization_barrier((a1, b1))
    a2, b2 = both(a1, "z", 8), halves(b1, "y", 4, 1)
    a2, b2 = lax.optimization_barrier((a2, b2))
    a3 = both(a2, "z", 8)
    narrow = [b0, b1[1], jnp.concatenate(b2, 1), b1[0]]
    narrow = jnp.concatenate([t.reshape(4, 1, 2, 32, NARROW) for t in narrow], 1)
    a3, narrow = lax.optimization_barrier((a3, narrow))
    a4 = halves(a3, "z", 8, 1)
    n1 = both((narrow, narrow), "z", 8)
    wide = [a0, a1[1], a2[1], a3[1], jnp.concatenate(a4, 1), a3[0], a2[0], a1[0]]
    wide = jnp.concatenate([t[:, None] for t in wide], 1)
    w1 = both((wide, wide), "y", 4)

    old = jnp.stack([master, momentum]).reshape(2, 4, 2, 160, 256)
    mine = lax.dynamic_index_in_dim(old, low, 2, keepdims=False)
    theirs = shift(after(lax.dynamic_index_in_dim(old, 1 - low, 2, keepdims=False), narrow), "xl", 2, 1)
    mine, theirs = mine.reshape(2, 640, 256), theirs.reshape(2, 640, 256)

    n2 = both(n1, "z", 8)
    w2 = halves(w1, "y", 4, 0)
    n3 = both(n2, "z", 8)
    shaped = lambda t: t.reshape(4, -1, t.shape[-1])
    tile = gradient(
        region_role,
        {0: shaped(wide), 1: shaped(w1[1]), 3: shaped(w1[0])},
        {0: shaped(narrow), 1: shaped(n1[1]), 7: shaped(n1[0]), 2: shaped(n2[1]), 6: shaped(n2[0])}, cots)
    n3, tile, theirs = lax.optimization_barrier((n3, tile, theirs))
    n4 = halves(n3, "z", 8, 0)
    own, other, rows = gradient(
        region_role,
        {2: shaped(jnp.concatenate(w2, 0))},
        {3: shaped(n3[1]), 5: shaped(n3[0]), 4: shaped(jnp.concatenate(n4, 0))}, cots, tile, (mine, theirs))

    came = shift(other, "xl", 2, 1)
    rows = lax.all_to_all(rows, ("y", "z"), split_axis=0, concat_axis=0, tiled=True)
    rows = rows.reshape(4, 8, 2, 20, 256).transpose(3, 0, 2, 1, 4).reshape(20, 16384)
    rollout_weight = every_region(rows, 0).reshape(4, 20, 16384)

    delta = in_order(low, own.reshape(4, 160, 256), came.reshape(4, 160, 256), 1).reshape(1280, 256)
    new_master, new_momentum = step(delta, master, momentum)
    learner_weight = lax.all_gather(new_master.astype(jnp.bfloat16), REGION, axis=0, tiled=True)
    return new_master, new_momentum, learner_weight, rollout_weight


def solution(mesh):
    fine = Mesh(mesh.devices.reshape(2, 2, 4, 2, 8), REGION + SHARD)
    tile = P(REGION, SHARD)
    return jax.shard_map(
        per_device,
        mesh=fine,
        in_specs=(P(), P(REGION + SHARD, None), tile, tile, tile),
        out_specs=(tile, tile, P(None, SHARD), P(None, SHARD, None)),
        check_vma=False,
    )
```

```python
import functools

import jax
import jax.numpy as jnp
from jax import lax
from jax.experimental import pallas as pl
from jax.experimental.pallas import tpu as pltpu
from jax.sharding import Mesh, PartitionSpec as P

REGION = ("xh", "core")
SHARD = ("y", "xl", "z")
WIDE = 384
NARROW = 256


def shift(x, axis, n, by):
    return lax.ppermute(x, axis, [(i, (i + by) % n) for i in range(n)])


def both(pair, axis, n):
    return shift(pair[0], axis, n, 1), shift(pair[1], axis, n, -1)


def halves(pair, axis, n, dim):
    size = pair[0].shape[dim] // 2
    return both(
        (lax.slice_in_dim(pair[0], 0, size, axis=dim), lax.slice_in_dim(pair[1], size, 2 * size, axis=dim)),
        axis, n)


def after(values, others):
    return lax.optimization_barrier((values, others))[0]


def gradient_kernel(js, ms, first, last, *refs):
    role, refs = refs[0], refs[1:]
    wide, refs = refs[: len(js)], refs[len(js) :]
    narrow, refs = refs[: len(ms)], refs[len(ms) :]
    cots, refs = refs[:2], refs[2:]
    before, refs = ((), refs) if first else (refs[:2], refs[2:])
    old, refs = (refs[:2], refs[2:]) if last else ((), refs)
    low, core = lax.axis_index("xl"), lax.axis_index("core")
    ys = [lax.rem(lax.axis_index("y") + j, 4) for j in range(4)]
    zs = [lax.rem(lax.axis_index("z") + m, 8) for m in range(8)]
    share = lambda r: jnp.where(role[r] < 2, 0.25, jnp.where(role[r] == 2, 0.5, 0.0))
    for side in range(2):
        column = low if side == 0 else 1 - low
        sources = [
            (cots[swapped].at[2 * high + column], 2 * high + (1 - core if swapped else core))
            for high in range(2) for swapped in range(2)]
        total = None if first else before[side][:WIDE, :]
        for cot, region in sources:
            for ref, j in zip(wide, js):
                rows = jnp.concatenate([cot[ys[j], l, zs[m]] for l in range(2) for m in range(8)], 0)
                part = share(region) * lax.dot_general(
                    ref[region], rows, (((0,), (0,)), ((), ())), preferred_element_type=jnp.float32)
                total = part if total is None else total + part
        refs[side][:WIDE, :] = total
        total = None if first else before[side][WIDE:, :]
        for cot, region in sources:
            for ref, m in zip(narrow, ms):
                rows = jnp.concatenate([cot[ys[j], l, zs[m]] for j in range(4) for l in range(2)], 0)
                part = share(region) * lax.dot_general(
                    ref[region], rows, (((0,), (0,)), ((), ())), preferred_element_type=jnp.float32)
                total = part if total is None else total + part
        refs[side][WIDE:, :] = total
        if last:
            for target in range(32):
                at = slice(20 * target, 20 * target + 20)
                new = step(refs[side][at, :], old[side][0, at, :], old[side][1, at, :])[0]
                refs[2][target, column] = new.astype(jnp.bfloat16)


def gradient(role, wide, narrow, cots, before=(), old=()):
    js, ms = tuple(wide), tuple(narrow)
    tile = jax.ShapeDtypeStruct((640, 256), jnp.float32)
    rows = jax.ShapeDtypeStruct((32, 2, 20, 256), jnp.bfloat16)
    operands = (role, *wide.values(), *narrow.values(), *cots, *before, *old)
    at = len(operands) - len(before) - len(old)
    share = (len(js) / 4 * WIDE + len(ms) / 8 * NARROW) / 640
    return pl.pallas_call(
        functools.partial(gradient_kernel, js, ms, not before, bool(old)),
        out_shape=(tile, tile, rows) if old else (tile, tile),
        in_specs=[pl.BlockSpec(memory_space=pltpu.SMEM)]
        + [pl.BlockSpec(memory_space=pltpu.VMEM)] * (len(operands) - 1),
        out_specs=[pl.BlockSpec(memory_space=pltpu.VMEM)] * (3 if old else 2),
        input_output_aliases={at: 0, at + 1: 1} if before else {},
        compiler_params=pltpu.CompilerParams(vmem_limit_bytes=16 << 20),
        cost_estimate=pl.CostEstimate(
            flops=int(share * 2 * 8192 * 640 * 512), bytes_accessed=int(share * (18 << 20)), transcendentals=0),
        name="gradient",
    )(*operands)


def step(delta, master, momentum):
    new_momentum = 0.9 * momentum + delta
    return master - 0.7 * (delta + 0.9 * new_momentum), new_momentum


def in_order(low, own, other, axis):
    return jnp.where(low == 0, jnp.stack([own, other], axis), jnp.stack([other, own], axis))


def every_region(block, axis):
    far, near = shift(block, "xh", 2, 1), shift(block, "core", 2, 1)
    far_near = shift(far, "core", 2, 1)
    core = lax.axis_index("core")
    return in_order(lax.axis_index("xh"), in_order(core, block, near, axis), in_order(core, far, far_near, axis), axis)


def per_device(region_role, tokens, cotangent, master, momentum):
    low, core = lax.axis_index("xl"), lax.axis_index("core")

    blocks = tokens.reshape(32, 4, 4, 2, 160).transpose(1, 3, 0, 2, 4).reshape(8, 32, 640)
    here = lax.all_to_all(blocks, ("xh", "core", "xl"), split_axis=0, concat_axis=0, tiled=True)
    a0, b0 = here[:, :, :WIDE], here[:, :, WIDE:]

    cots = jnp.broadcast_to(after(cotangent, here), (4, 2048, 256))
    cots = lax.all_to_all(cots, ("xh", "xl"), split_axis=0, concat_axis=0, tiled=True)

    a1, b1 = both((a0, a0), "z", 8), both((b0, b0), "y", 4)
    a1, b1 = lax.optimization_barrier((a1, b1))
    a2, b2 = both(a1, "z", 8), halves(b1, "y", 4, 1)
    a2, b2 = lax.optimization_barrier((a2, b2))
    a3 = both(a2, "z", 8)
    narrow = [b0, b1[1], jnp.concatenate(b2, 1), b1[0]]
    narrow = jnp.concatenate([t.reshape(4, 1, 2, 32, NARROW) for t in narrow], 1)
    a3, narrow = lax.optimization_barrier((a3, narrow))
    a4 = halves(a3, "z", 8, 1)
    n1 = both((narrow, narrow), "z", 8)
    wide = [a0, a1[1], a2[1], a3[1], jnp.concatenate(a4, 1), a3[0], a2[0], a1[0]]
    wide = jnp.concatenate([t[:, None] for t in wide], 1)
    w1 = both((wide, wide), "y", 4)

    old = jnp.stack([master, momentum]).reshape(2, 4, 2, 160, 256)
    mine = lax.dynamic_index_in_dim(old, low, 2, keepdims=False)
    theirs = shift(after(lax.dynamic_index_in_dim(old, 1 - low, 2, keepdims=False), narrow), "xl", 2, 1)
    mine, theirs = mine.reshape(2, 640, 256), theirs.reshape(2, 640, 256)

    n2 = both(n1, "z", 8)
    cots = after(cots, (w1, n2))
    swapped = shift(cots, "core", 2, 1)
    cots = [t.reshape(4, 4, 2, 8, 32, 256) for t in (cots, swapped)]
    w2 = halves(w1, "y", 4, 0)
    n3 = both(n2, "z", 8)
    shaped = lambda t: t.reshape(4, -1, t.shape[-1])
    tile = gradient(
        region_role,
        {0: shaped(wide), 1: shaped(w1[1]), 3: shaped(w1[0])},
        {0: shaped(narrow), 1: shaped(n1[1]), 7: shaped(n1[0]), 2: shaped(n2[1]), 6: shaped(n2[0])}, cots)
    n3, tile = lax.optimization_barrier((n3, tile))
    n4 = halves(n3, "z", 8, 0)
    own, other, rows = gradient(
        region_role,
        {2: shaped(jnp.concatenate(w2, 0))},
        {3: shaped(n3[1]), 5: shaped(n3[0]), 4: shaped(jnp.concatenate(n4, 0))}, cots, tile, (mine, theirs))

    came = shift(other, "xl", 2, 1)
    rows = lax.all_to_all(rows, ("y", "z"), split_axis=0, concat_axis=0, tiled=True)
    rows = rows.reshape(4, 8, 2, 20, 256).transpose(3, 0, 2, 1, 4).reshape(20, 16384)
    rollout_weight = every_region(rows, 0).reshape(4, 20, 16384)

    delta = in_order(low, own.reshape(4, 160, 256), came.reshape(4, 160, 256), 1).reshape(1280, 256)
    new_master, new_momentum = step(delta, master, momentum)
    learner_weight = every_region(new_master.astype(jnp.bfloat16), 0).reshape(5120, 256)
    return new_master, new_momentum, learner_weight, rollout_weight


def solution(mesh):
    fine = Mesh(mesh.devices.reshape(2, 2, 4, 2, 8), REGION + SHARD)
    tile = P(REGION, SHARD)
    return jax.shard_map(
        per_device,
        mesh=fine,
        in_specs=(P(), P(REGION + SHARD, None), tile, tile, tile),
        out_specs=(tile, tile, P(None, SHARD), P(None, SHARD, None)),
        check_vma=False,
    )
```

```python
import functools

import jax
import jax.numpy as jnp
from jax import lax
from jax.experimental import pallas as pl
from jax.experimental.pallas import tpu as pltpu
from jax.sharding import Mesh, PartitionSpec as P

REGION = ("xh", "core")
SHARD = ("y", "xl", "z")
WIDE = 384
NARROW = 256


def shift(x, axis, n, by):
    return lax.ppermute(x, axis, [(i, (i + by) % n) for i in range(n)])


def both(pair, axis, n):
    return shift(pair[0], axis, n, 1), shift(pair[1], axis, n, -1)


def halves(pair, axis, n, dim):
    size = pair[0].shape[dim] // 2
    return both(
        (lax.slice_in_dim(pair[0], 0, size, axis=dim), lax.slice_in_dim(pair[1], size, 2 * size, axis=dim)),
        axis, n)


def after(values, others):
    return lax.optimization_barrier((values, others))[0]


def gradient_kernel(js, ms, first, last, *refs):
    role, refs = refs[0], refs[1:]
    wide, refs = refs[: len(js)], refs[len(js) :]
    narrow, refs = refs[: len(ms)], refs[len(ms) :]
    cots, refs = refs[:2], refs[2:]
    before, refs = ((), refs) if first else (refs[:2], refs[2:])
    old, refs = (refs[:2], refs[2:]) if last else ((), refs)
    low, core = lax.axis_index("xl"), lax.axis_index("core")
    ys = [lax.rem(lax.axis_index("y") + j, 4) for j in range(4)]
    zs = [lax.rem(lax.axis_index("z") + m, 8) for m in range(8)]
    share = lambda r: jnp.where(role[r] < 2, 0.25, jnp.where(role[r] == 2, 0.5, 0.0))
    for side in range(2):
        column = low if side == 0 else 1 - low
        sources = [
            (cots[swapped].at[2 * high + column], 2 * high + (1 - core if swapped else core))
            for high in range(2) for swapped in range(2)]
        total = None if first else before[side][:WIDE, :]
        for cot, region in sources:
            for ref, j in zip(wide, js):
                rows = jnp.concatenate([cot[ys[j], l, zs[m]] for l in range(2) for m in range(8)], 0)
                part = share(region) * lax.dot_general(
                    ref[region], rows, (((0,), (0,)), ((), ())), preferred_element_type=jnp.float32)
                total = part if total is None else total + part
        refs[side][:WIDE, :] = total
        total = None if first else before[side][WIDE:, :]
        for cot, region in sources:
            for ref, m in zip(narrow, ms):
                rows = jnp.concatenate([cot[ys[j], l, zs[m]] for j in range(4) for l in range(2)], 0)
                part = share(region) * lax.dot_general(
                    ref[region], rows, (((0,), (0,)), ((), ())), preferred_element_type=jnp.float32)
                total = part if total is None else total + part
        refs[side][WIDE:, :] = total
        if last:
            for target in range(32):
                at = slice(20 * target, 20 * target + 20)
                new = moved(old[side][at, :], refs[side][at, :])
                refs[2][target, column] = new.astype(jnp.bfloat16)


def gradient(role, wide, narrow, cots, before=(), old=()):
    js, ms = tuple(wide), tuple(narrow)
    tile = jax.ShapeDtypeStruct((640, 256), jnp.float32)
    rows = jax.ShapeDtypeStruct((32, 2, 20, 256), jnp.bfloat16)
    operands = (role, *wide.values(), *narrow.values(), *cots, *before, *old)
    at = len(operands) - len(before) - len(old)
    share = (len(js) / 4 * WIDE + len(ms) / 8 * NARROW) / 640
    return pl.pallas_call(
        functools.partial(gradient_kernel, js, ms, not before, bool(old)),
        out_shape=(tile, tile, rows) if old else (tile, tile),
        in_specs=[pl.BlockSpec(memory_space=pltpu.SMEM)]
        + [pl.BlockSpec(memory_space=pltpu.VMEM)] * (len(operands) - 1),
        out_specs=[pl.BlockSpec(memory_space=pltpu.VMEM)] * (3 if old else 2),
        input_output_aliases={at: 0, at + 1: 1} if before else {},
        compiler_params=pltpu.CompilerParams(vmem_limit_bytes=16 << 20),
        cost_estimate=pl.CostEstimate(
            flops=int(share * 2 * 8192 * 640 * 512), bytes_accessed=int(share * (18 << 20)), transcendentals=0),
        name="gradient",
    )(*operands)


def moved(base, delta):
    return base - 1.33 * delta


def in_order(low, own, other, axis):
    return jnp.where(low == 0, jnp.stack([own, other], axis), jnp.stack([other, own], axis))


def every_region(block, axis):
    far, near = shift(block, "xh", 2, 1), shift(block, "core", 2, 1)
    far_near = shift(far, "core", 2, 1)
    core = lax.axis_index("core")
    return in_order(lax.axis_index("xh"), in_order(core, block, near, axis), in_order(core, far, far_near, axis), axis)


def per_device(region_role, tokens, cotangent, master, momentum):
    low, core = lax.axis_index("xl"), lax.axis_index("core")

    blocks = tokens.reshape(32, 4, 4, 2, 160).transpose(1, 3, 0, 2, 4).reshape(8, 32, 640)
    here = lax.all_to_all(blocks, ("xh", "core", "xl"), split_axis=0, concat_axis=0, tiled=True)
    a0, b0 = here[:, :, :WIDE], here[:, :, WIDE:]

    cots = jnp.broadcast_to(after(cotangent, here), (4, 2048, 256))
    cots = lax.all_to_all(cots, ("xh", "xl"), split_axis=0, concat_axis=0, tiled=True)

    a1, b1 = both((a0, a0), "z", 8), both((b0, b0), "y", 4)
    a1, b1 = lax.optimization_barrier((a1, b1))
    a2, b2 = both(a1, "z", 8), halves(b1, "y", 4, 1)
    a2, b2 = lax.optimization_barrier((a2, b2))
    a3 = both(a2, "z", 8)
    narrow = [b0, b1[1], jnp.concatenate(b2, 1), b1[0]]
    narrow = jnp.concatenate([t.reshape(4, 1, 2, 32, NARROW) for t in narrow], 1)
    a3, narrow = lax.optimization_barrier((a3, narrow))
    a4 = halves(a3, "z", 8, 1)
    n1 = both((narrow, narrow), "z", 8)
    wide = [a0, a1[1], a2[1], a3[1], jnp.concatenate(a4, 1), a3[0], a2[0], a1[0]]
    wide = jnp.concatenate([t[:, None] for t in wide], 1)
    w1 = both((wide, wide), "y", 4)

    base = master - 0.567 * momentum
    old = base.reshape(4, 2, 160, 256)
    mine = lax.dynamic_index_in_dim(old, low, 1, keepdims=False)
    theirs = shift(after(lax.dynamic_index_in_dim(old, 1 - low, 1, keepdims=False), narrow), "xl", 2, 1)
    mine, theirs = mine.reshape(640, 256), theirs.reshape(640, 256)

    n2 = both(n1, "z", 8)
    cots = after(cots, (w1, n2))
    swapped = shift(cots, "core", 2, 1)
    cots = [t.reshape(4, 4, 2, 8, 32, 256) for t in (cots, swapped)]
    w2 = halves(w1, "y", 4, 0)
    n3 = both(n2, "z", 8)
    shaped = lambda t: t.reshape(4, -1, t.shape[-1])
    tile = gradient(
        region_role,
        {0: shaped(wide), 1: shaped(w1[1]), 3: shaped(w1[0])},
        {0: shaped(narrow), 1: shaped(n1[1]), 7: shaped(n1[0]), 2: shaped(n2[1]), 6: shaped(n2[0])}, cots)
    n3, tile = lax.optimization_barrier((n3, tile))
    n4 = halves(n3, "z", 8, 0)
    own, other, rows = gradient(
        region_role,
        {2: shaped(jnp.concatenate(w2, 0))},
        {3: shaped(n3[1]), 5: shaped(n3[0]), 4: shaped(jnp.concatenate(n4, 0))}, cots, tile, (mine, theirs))

    came = shift(other, "xl", 2, 1)
    rows = lax.all_to_all(rows, ("y", "z"), split_axis=0, concat_axis=0, tiled=True)
    rows = rows.reshape(4, 8, 2, 20, 256).transpose(3, 0, 2, 1, 4).reshape(20, 16384)
    rollout_weight = every_region(rows, 0).reshape(4, 20, 16384)

    delta = in_order(low, own.reshape(4, 160, 256), came.reshape(4, 160, 256), 1).reshape(1280, 256)
    new_master, new_momentum = moved(base, delta), 0.9 * momentum + delta
    learner_weight = every_region(new_master.astype(jnp.bfloat16), 0).reshape(5120, 256)
    return new_master, new_momentum, learner_weight, rollout_weight


def solution(mesh):
    fine = Mesh(mesh.devices.reshape(2, 2, 4, 2, 8), REGION + SHARD)
    tile = P(REGION, SHARD)
    return jax.shard_map(
        per_device,
        mesh=fine,
        in_specs=(P(), P(REGION + SHARD, None), tile, tile, tile),
        out_specs=(tile, tile, P(None, SHARD), P(None, SHARD, None)),
        check_vma=False,
    )
```
